768 devices in a mesh: stream: 96 (over y, z), cross: 8 (over x, core).
Axes of the slice: x: 4, y: 8, z: 12, core: 2. Of those that a mesh axis runs over, the one named last changes fastest.
Arguments:
- fluid_state: float32 [5, 768, 64, 128], P(None, 'stream', 'cross'), may hold values from -6 to 6
- drop_xi: float32 [3, 96, 8, 8, 128], P(None, 'stream', 'cross'), may hold values from -1 to 1
- drop_vel: float32 [3, 96, 8, 8, 128], P(None, 'stream', 'cross'), may hold values from -4 to 4
- drop_tau: float32 [96, 8, 8, 128], P('stream', 'cross'), may hold values from 0.02 to 0.2
- drop_mass: float32 [96, 8, 8, 128], P('stream', 'cross'), may hold values from 0.5 to 5
- drop_host: int32 [96, 8, 8, 128], P('stream', 'cross'), may hold values from 0 to 15, as said below
- drop_alive: int32 [96, 8, 8, 128], P('stream', 'cross'), may hold values from 0 to 1, as said below
- depart_slots: int32 [96, 8, 256], P('stream', 'cross'), may hold values from 0 to 1023, as said below
- depart_count: int32 [96, 8], P('stream', 'cross'), may hold values from 0 to 256, as said below
- arrive_slots: int32 [96, 8, 256], P('stream', 'cross'), may hold values from 0 to 1023, as said below
- arrive_host: int32 [96, 8, 256], P('stream', 'cross'), may hold values from 0 to 15, as said below
- arrive_count: int32 [96, 8], P('stream', 'cross'), may hold values from 0 to 256, as said below
Outputs:
- new_state: float32 [5, 768, 64, 128], P(None, 'stream', 'cross')
- new_register: float32 [5, 768, 64, 128], P(None, 'stream', 'cross')
- drop_velocity: float32 [3, 96, 8, 8, 128], P(None, 'stream', 'cross')
- drop_register: float32 [3, 96, 8, 8, 128], P(None, 'stream', 'cross')
The draws below stay inside these ranges and needn't reach their ends.
Inputs may be any that keep to these rules, and one draw needn't show every extreme that they name: `drop_host`: element of the slot's droplet among the 16 elements of its owner, numbered (a + e) * 16 + z by element coordinates; every departing droplet lies in the layer a = 0. `drop_alive`: every listed departure is live and every listed arrival slot is empty before it arrives. `depart_slots`: the first depart_count entries are distinct slots numbered block * 128 + slot, at most 32 of them in one block. `depart_count`: some device reaches 256. `arrive_slots`: the first arrive_count entries are distinct slots, entry i in the same block as entry i of the departure list of the previous slab's device with the same cross index. `arrive_host`: arriving droplets lie in the first element layer, the departing element's other coordinates kept. `arrive_count`: equals the departure count of the previous slab's device with the same cross index; zero on the first slab.
All inputs are finite; a program needn't handle non-finite values.
Results may differ from the reference program's by a relative error of at most 0.0003.
Values sent between devices are 32-bit elements; how exact they have to be, the bound alone decides.
No kernel may reach another device: no remote copies, remote signals or barrier semaphores. Data moves between devices by JAX's collectives and lax.ppermute only.
A program may use at most 64 MiB of HBM per device.

```python
import math
import jax
import jax.numpy as jnp
import numpy as np
from jax import lax

NVAR = 5
EX = 1
EC = 1
EZ = 16
CAP = 128
MB = 32
SLABS = 96
GROUP = 8
ELEM = 16
K = 256
NX = 768
NY = 64
NZ = 128


def droplet_plan(key):
    root_key = jax.random.fold_in(key, 4242)
    subkeys = jax.random.split(root_key, 5)
    grid_shape = (SLABS, GROUP, GROUP, CAP)
    scores = jax.random.randint(subkeys[0], grid_shape, 0, 2 ** 16) * CAP + jnp.arange(CAP, dtype=jnp.int32)
    permuted = jnp.argsort(scores, axis=-1, stable=True).astype(jnp.int32)
    ranking = jnp.argsort(permuted, axis=-1, stable=True).astype(jnp.int32)
    block_ix = jnp.arange(GROUP, dtype=jnp.int32)
    distance = jnp.abs(2 * block_ix - (GROUP - 1))
    alive_limit = 950 - 800 * distance // GROUP
    base_alive = (jax.random.randint(subkeys[1], grid_shape, 0, 1000) < alive_limit[None, None, :, None]).astype(jnp.int32)
    host_draw = jax.random.randint(subkeys[2], grid_shape, 0, ELEM)
    counts = jax.random.randint(subkeys[3], (SLABS, GROUP, GROUP), 0, MB + 1)
    chosen = jax.random.randint(subkeys[4], (), 0, (SLABS - 1) * GROUP)
    device_ix = jnp.arange(SLABS)[:, None] * GROUP + jnp.arange(GROUP)[None, :]
    counts = jnp.where((device_ix == chosen)[:, :, None], MB, counts)
    previous = jnp.concatenate([jnp.zeros_like(counts[:1]), counts[:-1]], axis=0)
    leaving = ranking < counts[..., None]
    landing = ranking >= CAP - previous[..., None]
    last_layer = ((EX - 1) * EC + host_draw // EZ % EC) * EZ + host_draw % EZ
    host_ids = jnp.where(leaving, last_layer, host_draw).astype(jnp.int32)
    alive_mask = jnp.where(leaving, 1, jnp.where(landing, 0, base_alive)).astype(jnp.int32)
    lane_ix = jnp.arange(MB, dtype=jnp.int32)
    flat_src = (block_ix[None, None, :, None] * CAP + permuted[..., :MB]).reshape(SLABS, GROUP, K)
    usable = (lane_ix[None, None, None, :] < counts[..., None]).reshape(SLABS, GROUP, K).astype(jnp.int32)
    sorting = jnp.argsort(1 - usable, axis=-1, stable=True).astype(jnp.int32)
    depart_slots = jnp.take_along_axis(flat_src, sorting, axis=-1).astype(jnp.int32)
    depart_count = jnp.sum(usable, axis=-1).astype(jnp.int32)
    land_slot = (block_ix[None, None, :, None] * CAP + jnp.take(permuted, CAP - 1 - lane_ix, axis=-1)).reshape(SLABS, GROUP, K)
    sender_host = jnp.take_along_axis(host_ids.reshape(SLABS, GROUP, GROUP * CAP), flat_src, axis=-1) - (EX - 1) * EC * EZ
    prior_sorting = jnp.concatenate([jnp.zeros_like(sorting[:1]), sorting[:-1]], axis=0)
    prior_host = jnp.concatenate([jnp.zeros_like(sender_host[:1]), sender_host[:-1]], axis=0)
    arrive_slots = jnp.take_along_axis(land_slot, prior_sorting, axis=-1).astype(jnp.int32)
    arrive_host = jnp.take_along_axis(prior_host, prior_sorting, axis=-1).astype(jnp.int32)
    arrive_count = jnp.concatenate([jnp.zeros_like(depart_count[:1]), depart_count[:-1]], axis=0).astype(jnp.int32)
    return (host_ids, alive_mask, depart_slots, depart_count, arrive_slots, arrive_host, arrive_count)


def draw_drop_host(key, part):
    return droplet_plan(key)[0]


def draw_drop_alive(key, part):
    return droplet_plan(key)[1]


def draw_depart_slots(key, part):
    return droplet_plan(key)[2]


def draw_depart_count(key, part):
    return droplet_plan(key)[3]


def draw_arrive_slots(key, part):
    return droplet_plan(key)[4]


def draw_arrive_host(key, part):
    return droplet_plan(key)[5]


def draw_arrive_count(key, part):
    return droplet_plan(key)[6]


def level_of(key, shape, shards, least, largest):
    level, own = 1.0, jax.random.fold_in(key, 6)
    for dim, shards_of in shards:
        draws = jnp.exp(jax.random.uniform(jax.random.fold_in(own, dim), (shards_of,), jnp.float32, least / len(shards), largest / len(shards)))
        level = level * jnp.repeat(draws, shape[dim] // shards_of).reshape([-1 if axis == dim else 1 for axis in range(len(shape))])
    return level


def noise(key, dims, scale, bound, cuts=(), kind=jnp.bfloat16):
    factor_of = level_of(key, dims, cuts, -0.22, 0.18) if cuts else 1.0
    values = jax.random.normal(key, dims, jnp.float32) * scale * factor_of
    return jnp.minimum(jnp.maximum(values, -bound), bound).astype(kind)


def setup_inputs(seed: int = 0) -> dict:
    keys = jax.random.split(jax.random.key(seed), 13)
    fluid_state = noise(keys[0], (NVAR, NX, NY, NZ), 1.0, 6.0, ((1, 96), (2, 8)), jnp.float32)
    drop_xi = jnp.clip(jax.random.uniform(keys[1], (3, SLABS, GROUP, GROUP, CAP), jnp.float32, -1.0, 1.0) * level_of(keys[1], (3, SLABS, GROUP, GROUP, CAP), ((1, 96), (2, 8)), -0.4, 0.0), -1.0, 1.0)
    drop_vel = noise(keys[2], (3, SLABS, GROUP, GROUP, CAP), 0.5, 4.0, ((1, 96), (2, 8)), jnp.float32)
    drop_tau = jnp.clip(jnp.exp(math.log(0.2) - 2.3025851 * jax.random.uniform(keys[3], (SLABS, GROUP, GROUP, CAP), jnp.float32) ** level_of(keys[3], (SLABS, GROUP, GROUP, CAP), ((0, 96), (1, 8)), -0.2, 0.2)), 0.02, 0.2)
    drop_mass = jnp.clip(jnp.exp(math.log(5.0) - 2.3025851 * jax.random.uniform(keys[4], (SLABS, GROUP, GROUP, CAP), jnp.float32) ** level_of(keys[4], (SLABS, GROUP, GROUP, CAP), ((0, 96), (1, 8)), -0.2, 0.2)), 0.5, 5.0)
    drop_host = draw_drop_host(jax.random.fold_in(keys[12], 71), 0)
    drop_alive = draw_drop_alive(jax.random.fold_in(keys[12], 71), 0)
    depart_slots = draw_depart_slots(jax.random.fold_in(keys[12], 71), 0)
    depart_count = draw_depart_count(jax.random.fold_in(keys[12], 71), 0)
    arrive_slots = draw_arrive_slots(jax.random.fold_in(keys[12], 71), 0)
    arrive_host = draw_arrive_host(jax.random.fold_in(keys[12], 71), 0)
    arrive_count = draw_arrive_count(jax.random.fold_in(keys[12], 71), 0)
    return {"fluid_state": fluid_state, "drop_xi": drop_xi, "drop_vel": drop_vel, "drop_tau": drop_tau, "drop_mass": drop_mass, "drop_host": drop_host, "drop_alive": drop_alive, "depart_slots": depart_slots, "depart_count": depart_count, "arrive_slots": arrive_slots, "arrive_host": arrive_host, "arrive_count": arrive_count}


SPEED = 2.0
LIFT = 28.0
STEP_SIZE = 0.02
COEF_A = (0.0, -567301805773.0 / 1357537059087.0)
COEF_B = (1432997174477.0 / 9575080441755.0, 5161836677717.0 / 13612068292357.0)


def lgl_tables():
    node_pos = np.array([-1.0, -0.871740148509607, -0.591700181433142, -0.209299217902479,
                         0.209299217902479, 0.591700181433142, 0.871740148509607, 1.0])
    bary_wts = np.array([1.0 / np.prod([node_pos[a] - node_pos[b] for b in range(8) if b != a]) for a in range(8)])
    deriv_mat = np.zeros((8, 8))
    for a in range(8):
        for b in range(8):
            if a != b:
                deriv_mat[a, b] = (bary_wts[b] / bary_wts[a]) / (node_pos[a] - node_pos[b])
        deriv_mat[a, a] = -np.sum(deriv_mat[a])
    return node_pos, bary_wts, deriv_mat


def jet_profile(cell_rows, first_el, width_el):
    node_pos = lgl_tables()[0]
    el_index = (first_el + jnp.arange(cell_rows // 8)).astype(jnp.float32)
    offsets = jnp.asarray(0.5 * (1.0 + node_pos), dtype=jnp.float32)
    coord_y = (el_index[:, None] + offsets[None, :]).reshape(cell_rows)
    center = 0.5 * width_el
    radius = 0.25 * width_el
    return 0.1 + 0.4 * (1.0 + jnp.tanh(2.0 * (radius - jnp.abs(coord_y - center))))


def flux_along(flow_field, mean_flow, direction):
    density, vel_x, vel_y, vel_z, pressure = flow_field[0], flow_field[1], flow_field[2], flow_field[3], flow_field[4]
    zero_part = jnp.zeros_like(density)
    if direction == 0:
        components = [mean_flow * density + vel_x, mean_flow * vel_x + pressure, mean_flow * vel_y,
                      mean_flow * vel_z, mean_flow * pressure + vel_x]
    elif direction == 1:
        components = [vel_y, zero_part, pressure, zero_part, vel_y]
    else:
        components = [vel_z, zero_part, zero_part, pressure, vel_z]
    return jnp.stack(components)


def direction_term(flow_field, low_ghost, high_ghost, mean_flow, direction):
    deriv_mat = lgl_tables()[2]
    axis_pos = direction + 1
    shape_in = flow_field.shape
    count_el = shape_in[axis_pos] // 8
    split_shape = shape_in[:axis_pos] + (count_el, 8) + shape_in[axis_pos + 1:]
    split_flux = flux_along(flow_field, mean_flow, direction).reshape(split_shape)
    split_field = flow_field.reshape(split_shape)
    einsum_forms = ["ij,vejyz->veiyz", "ij,vxejz->vxeiz", "ij,vxyej->vxyei"]
    volume = jnp.einsum(einsum_forms[direction], jnp.asarray(deriv_mat, dtype=flow_field.dtype), split_flux,
                        precision=lax.Precision.HIGHEST)
    first_idx = (slice(None),) * (axis_pos + 1) + (0,)
    last_idx = (slice(None),) * (axis_pos + 1) + (7,)
    left_states = jnp.concatenate([low_ghost, split_field[last_idx]], axis=axis_pos)
    right_states = jnp.concatenate([split_field[first_idx], high_ghost], axis=axis_pos)
    face_flux = 0.5 * (flux_along(left_states, mean_flow, direction) + flux_along(right_states, mean_flow, direction)) \
        - 0.5 * SPEED * (right_states - left_states)
    low_face = lax.slice_in_dim(face_flux, 0, count_el, axis=axis_pos)
    high_face = lax.slice_in_dim(face_flux, 1, count_el + 1, axis=axis_pos)
    lift_low = (low_face - split_flux[first_idx]) * LIFT
    lift_high = (high_face - split_flux[last_idx]) * LIFT
    result = (-volume).at[first_idx].add(lift_low).at[last_idx].add(-lift_high)
    return result.reshape(shape_in)


def fluid_rate(flow_field, low_x, high_x, low_y, high_y, mean_flow):
    term_x = direction_term(flow_field, low_x, high_x, mean_flow, 0)
    term_y = direction_term(flow_field, low_y, high_y, mean_flow, 1)
    term_z = direction_term(flow_field, flow_field[..., -1:], flow_field[..., :1], mean_flow, 2)
    return term_x + term_y + term_z


def basis_rows(coords):
    node_pos, bary_wts, _ = lgl_tables()
    factors = []
    for axis_no in range(3):
        coord_row = coords[axis_no]
        values = []
        for node_a in range(8):
            product_term = jnp.full_like(coord_row, float(bary_wts[node_a]))
            for node_b in range(8):
                if node_b != node_a:
                    product_term = product_term * (coord_row - float(node_pos[node_b]))
            values.append(product_term)
        factors.append(jnp.stack(values, axis=1))
    weights = factors[0][:, :, None, None] * factors[1][:, None, :, None] * factors[2][:, None, None, :]
    return weights.reshape(coords.shape[1], 512)


def sample_fluid(elem_table, row_ids, weights):
    picked = elem_table[row_ids]
    return jnp.sum(picked * weights[:, None, :], axis=-1).T


def spread_force(deposit, row_ids, weights, force):
    contrib = -(force.T[:, :, None] * weights[:, None, :])
    return deposit.at[row_ids].add(contrib)


def droplet_forces(flow_field, mean_flow, coords, velocity, relax_time, mass_load, host_ids):
    vel_three = jnp.stack([mean_flow + flow_field[1], flow_field[2], flow_field[3]])
    elem_table = vel_three.reshape(3, SLABS, EX, 8, GROUP, EC, 8, EZ, 8).transpose(1, 4, 2, 5, 7, 0, 3, 6, 8)
    elem_table = elem_table.reshape(SLABS, GROUP * ELEM, 3, 512)
    owner_rows = ((jnp.arange(GROUP * CAP) // CAP) * ELEM).astype(jnp.int32)

    def step(deposit, inputs):
        device_no, step_xi, step_vel, step_tau, step_load, step_host = inputs
        slab_no = device_no // GROUP
        row_ids = owner_rows + step_host
        weights = basis_rows(step_xi)
        fluid_at = sample_fluid(elem_table[slab_no], row_ids, weights)
        tendency = (fluid_at - step_vel) / step_tau
        deposit = deposit.at[slab_no].set(spread_force(deposit[slab_no], row_ids, weights, step_load * tendency))
        return deposit, tendency

    deposit, accel = lax.scan(step, jnp.zeros_like(elem_table),
                              (jnp.arange(SLABS * GROUP).astype(jnp.int32), coords, velocity, relax_time, mass_load, host_ids))
    source = deposit.reshape(SLABS, GROUP, EX, EC, EZ, 3, 8, 8, 8).transpose(5, 0, 2, 6, 1, 3, 7, 4, 8)
    return source.reshape(3, NX, NY, NZ), accel


def pack_leaving(coords, velocity, register, relax_time, drop_mass, depart_slots):
    return jnp.concatenate([coords[:, depart_slots], velocity[:, depart_slots], register[:, depart_slots],
                            relax_time[depart_slots][None], drop_mass[depart_slots][None]], axis=0)


def clear_leaving(alive_mask, depart_slots, depart_count):
    lane_ix = jnp.arange(depart_slots.shape[0])
    target = jnp.where(lane_ix < depart_count, depart_slots, alive_mask.shape[0])
    return alive_mask.at[target].set(0, mode="drop")


def land_arriving(coords, velocity, register, relax_time, drop_mass, host_ids, alive_mask, incoming,
                  arrive_slots, arrive_host, arrive_count):
    lane_ix = jnp.arange(arrive_slots.shape[0])
    target = jnp.where(lane_ix < arrive_count, arrive_slots, host_ids.shape[0])
    coords = coords.at[:, target].set(incoming[0:3], mode="drop")
    velocity = velocity.at[:, target].set(incoming[3:6], mode="drop")
    register = register.at[:, target].set(incoming[6:9], mode="drop")
    relax_time = relax_time.at[target].set(incoming[9], mode="drop")
    drop_mass = drop_mass.at[target].set(incoming[10], mode="drop")
    host_ids = host_ids.at[target].set(arrive_host, mode="drop")
    alive_mask = alive_mask.at[target].set(1, mode="drop")
    return coords, velocity, register, relax_time, drop_mass, host_ids, alive_mask


def reference(fluid_state, drop_xi, drop_vel, drop_tau, drop_mass, drop_host, drop_alive,
              depart_slots, depart_count, arrive_slots, arrive_host, arrive_count):
    devices = SLABS * GROUP
    slot_count = GROUP * CAP
    mean_flow = jet_profile(NY, 0, NY // 8)[None, :, None]
    coords = drop_xi.reshape(3, devices, slot_count).transpose(1, 0, 2)
    velocity = drop_vel.reshape(3, devices, slot_count).transpose(1, 0, 2)
    relax_time = drop_tau.reshape(devices, slot_count)
    mass_raw = drop_mass.reshape(devices, slot_count)
    host_ids = drop_host.reshape(devices, slot_count)
    alive_mask = drop_alive.reshape(devices, slot_count)
    leave_slots = depart_slots.reshape(devices, K)
    leave_count = depart_count.reshape(devices)
    land_slots = arrive_slots.reshape(devices, K)
    land_host = arrive_host.reshape(devices, K)
    land_count = arrive_count.reshape(devices)
    flow_field = fluid_state
    register = jnp.zeros_like(fluid_state)
    drop_reg = jnp.zeros_like(velocity)
    for section_no in range(2):
        padded = jnp.pad(flow_field, ((0, 0), (1, 1), (1, 1), (0, 0)))
        tendency = fluid_rate(flow_field, padded[:, :1, 1:-1], padded[:, -1:, 1:-1],
                              padded[:, 1:-1, :1], padded[:, 1:-1, -1:], mean_flow)
        mass_load = mass_raw * alive_mask.astype(jnp.float32)
        source, accel = droplet_forces(flow_field, mean_flow, coords, velocity, relax_time, mass_load, host_ids)
        tendency = tendency.at[1:4].add(source)
        register = COEF_A[section_no] * register + STEP_SIZE * tendency
        flow_field = flow_field + COEF_B[section_no] * register
        drop_reg = COEF_A[section_no] * drop_reg + STEP_SIZE * accel
        velocity = velocity + COEF_B[section_no] * drop_reg
        if section_no == 0:
            packed = jax.vmap(pack_leaving)(coords, velocity, drop_reg, relax_time, mass_raw, leave_slots)
            alive_mask = jax.vmap(clear_leaving)(alive_mask, leave_slots, leave_count)
            packed = packed.reshape(SLABS, GROUP, 11, K)
            incoming = jnp.concatenate([jnp.zeros_like(packed[:1]), packed[:-1]], axis=0).reshape(devices, 11, K)
            coords, velocity, drop_reg, relax_time, mass_raw, host_ids, alive_mask = jax.vmap(land_arriving)(
                coords, velocity, drop_reg, relax_time, mass_raw, host_ids, alive_mask, incoming,
                land_slots, land_host, land_count)
    live = alive_mask.astype(jnp.float32)[:, None, :]
    drop_velocity = (velocity * live).transpose(1, 0, 2).reshape(3, SLABS, GROUP, GROUP, CAP)
    drop_register = (drop_reg * live).transpose(1, 0, 2).reshape(3, SLABS, GROUP, GROUP, CAP)
    return flow_field, register, drop_velocity, drop_register
```

```python
import jax
import jax.numpy as jnp
import numpy as np
from jax import lax
from jax.experimental import pallas as pl
from jax.experimental.pallas import tpu as pltpu
from jax.sharding import PartitionSpec as P

LIFT = 28.0
STEP_SIZE = 0.02
COEF_A = (0.0, -567301805773.0 / 1357537059087.0)
COEF_B = (1432997174477.0 / 9575080441755.0, 5161836677717.0 / 13612068292357.0)
F32 = jnp.float32
BF16 = jnp.bfloat16

TAU, LOAD, HOST, OUT_POS, IN_POS, IN_HOST, ALIVE = 6, 7, 8, 9, 10, 11, 12
PLANES = 16


def lgl_tables():
    node_pos = np.array(
        [
            -1.0,
            -0.871740148509607,
            -0.591700181433142,
            -0.209299217902479,
            0.209299217902479,
            0.591700181433142,
            0.871740148509607,
            1.0,
        ]
    )
    bary_wts = np.array(
        [1.0 / np.prod([node_pos[a] - node_pos[b] for b in range(8) if b != a]) for a in range(8)]
    )
    deriv_mat = np.zeros((8, 8))
    for a in range(8):
        for b in range(8):
            if a != b:
                deriv_mat[a, b] = bary_wts[b] / bary_wts[a] / (node_pos[a] - node_pos[b])
        deriv_mat[a, a] = -np.sum(deriv_mat[a])
    return (node_pos, bary_wts, deriv_mat)


NODES, BARY, DERIV = lgl_tables()


def column_planes():
    rows = [BARY]
    rows += [np.roll(NODES, -t) for t in range(1, 8)]
    rows += [-DERIV[:, j] for j in range(8)]
    rows += [0.5 * (1.0 + NODES)]
    rows += [LIFT * (np.arange(8) == 0), LIFT * (np.arange(8) == 7)]
    table = np.stack(rows).astype(np.float32)
    return np.ascontiguousarray(np.broadcast_to(table[:, :, None], table.shape + (128,)))


def span_matrix():
    full = np.zeros((128, 128))
    for e in range(16):
        base = 8 * e
        full[base : base + 8, base : base + 8] -= DERIV.T
        full[(base - 1) % 128, base] += 0.5 * LIFT
        full[base, base] -= 0.5 * LIFT
        full[(base + 8) % 128, base + 7] -= 0.5 * LIFT
        full[base + 7, base + 7] += 0.5 * LIFT
    high = full.astype(np.float32).astype(jnp.bfloat16)
    low = (full - high.astype(np.float64)).astype(np.float32).astype(jnp.bfloat16)
    return np.concatenate([high, high, low], axis=0)


def two_parts(values):
    high = values.astype(BF16)
    return high, (values - high.astype(F32)).astype(BF16)


def three_parts(values):
    high = values.astype(BF16)
    rest = values - high.astype(F32)
    mid = rest.astype(BF16)
    low = (rest - mid.astype(F32)).astype(BF16)
    return jnp.concatenate([high, mid, low], axis=0)


def dot_rows(left, right):
    return lax.dot_general(left, right, (((1,), (1,)), ((), ())), preferred_element_type=F32)


def dot_plain(left, right):
    return lax.dot_general(left, right, (((1,), (0,)), ((), ())), preferred_element_type=F32)


def row(values, index):
    return jnp.broadcast_to(values[index : index + 1], (8, values.shape[1]))


def flag(mask):
    return jnp.where(mask, 1.0, 0.0)


def mean_profile(cols):
    width = float(lax.axis_size("cross"))
    coord_y = lax.axis_index("cross").astype(F32) + cols[16]
    return 0.1 + 0.4 * (1.0 + jnp.tanh(2.0 * (0.25 * width - jnp.abs(coord_y - 0.5 * width))))


def basis(coord_row, cols):
    coord = jnp.broadcast_to(coord_row, (8, 128))
    value = cols[0] * (coord - cols[1])
    for t in range(2, 8):
        value = value * (coord - cols[t])
    return value


def list_planes(dep, dep_count, arr, arr_host, arr_count):
    lanes = dep.shape[1]
    lane = lax.broadcasted_iota(jnp.int32, (1, lanes), 1)
    block_no = lax.broadcasted_iota(jnp.int32, (8, lanes), 0)
    slot_no = lax.broadcasted_iota(jnp.int32, (128, lanes), 0)

    def member(slots, count):
        block = jnp.where(lane < count, slots >> 7, -1)
        return flag(block_no == block)

    dep_in, arr_in = member(dep, dep_count), member(arr, arr_count)
    earlier = flag(
        lax.broadcasted_iota(jnp.int32, (lanes, lanes), 0)
        < lax.broadcasted_iota(jnp.int32, (lanes, lanes), 1)
    ).astype(BF16)
    both = jnp.concatenate([dep_in, arr_in], axis=0)
    ranks = both * (dot_plain(both.astype(BF16), earlier) + 1.0)
    dep_hot = flag(slot_no == (dep & 127)).astype(BF16)
    arr_hot = flag(slot_no == (arr & 127)).astype(BF16)
    out_pos = dot_rows(ranks[:8].astype(BF16), dep_hot)
    arr_rows = jnp.concatenate([ranks[8:], arr_in * arr_host.astype(F32)], axis=0)
    landed = dot_rows(arr_rows.astype(BF16), arr_hot)
    return out_pos, landed[:8], landed[8:]


def send_kernel(
    state, xi, vel, tau, mass, host, alive, dep, dep_count, arr, arr_host, arr_count,
    out, x_first, x_last, y_first, y_last,
):
    x_first[...] = state[:, 0]
    x_last[...] = state[:, 7]
    y_first[...] = state[:, :, 0, :]
    y_last[...] = state[:, :, 7, :]
    live = alive[...].astype(F32)
    out_pos, in_pos, in_host = list_planes(
        dep[...], dep_count[0, 0], arr[...], arr_host[...], arr_count[0, 0]
    )
    for a in range(3):
        out[:, a, :] = xi[a]
        out[:, 3 + a, :] = vel[a]
    out[:, TAU, :] = tau[...]
    out[:, LOAD, :] = mass[...] * live
    out[:, HOST, :] = host[...].astype(F32)
    out[:, OUT_POS, :] = out_pos
    out[:, IN_POS, :] = in_pos
    out[:, IN_HOST, :] = in_host
    out[:, ALIVE, :] = live
    for r in range(ALIVE + 1, PLANES):
        out[:, r, :] = jnp.zeros((8, 128), F32)


def fill_weights(c, coords, host_row, cols, w, l1, l2):
    lanes = pl.ds(128 * c, 128)
    l1[:, lanes] = basis(coords[0:1], cols)
    l2[:, lanes] = basis(coords[1:2], cols)
    third = basis(coords[2:3], cols)
    high = third.astype(BF16).astype(F32)
    low = third - high
    host = jnp.broadcast_to(host_row, (8, 128))
    zero = jnp.zeros((8, 128), F32)
    for e in range(0, 16, 2):
        here, after = host == float(e), host == float(e + 1)
        rows_h = jnp.concatenate(
            [jnp.where(here, high, zero), jnp.where(after, high, zero)], axis=0
        ).astype(BF16)
        rows_l = jnp.concatenate(
            [jnp.where(here, low, zero), jnp.where(after, low, zero)], axis=0
        ).astype(BF16)
        w[pl.ds(8 * e, 16), lanes] = rows_h
        w[pl.ds(128 + 8 * e, 16), lanes] = rows_h
        w[pl.ds(256 + 8 * e, 16), lanes] = rows_l


def sample_all(state, mean_flow, w, s):
    fields = jnp.concatenate([state[1] + mean_flow[None], state[2], state[3]], axis=0)
    high, low = two_parts(fields.reshape(192, 128))
    s[...] = dot_plain(jnp.concatenate([high, low, high], axis=1), w[...])


def fluid_rows(c, s, l1, l2):
    lanes = pl.ds(128 * c, 128)
    along_x, along_y = l1[:, lanes], l2[:, lanes]
    rows = []
    for a in range(3):
        total = None
        for i in range(8):
            term = row(along_x, i) * s[pl.ds(64 * a + 8 * i, 8), lanes]
            total = term if total is None else total + term
        rows.append(jnp.sum(total * along_y, axis=0, keepdims=True))
    return jnp.concatenate(rows, axis=0)


def fill_force(c, force, l1, l2, fh, fl):
    lanes = pl.ds(128 * c, 128)
    along_x, along_y = l1[:, lanes], l2[:, lanes]
    pushes = [-row(force, a) for a in range(3)]
    for i in range(0, 8, 2):
        plane = jnp.concatenate([row(along_x, i) * along_y, row(along_x, i + 1) * along_y], axis=0)
        for a in range(3):
            high, low = two_parts(plane * jnp.concatenate([pushes[a], pushes[a]], axis=0))
            fh[pl.ds(64 * a + 8 * i, 16), lanes] = high
            fl[pl.ds(64 * a + 8 * i, 16), lanes] = low


def deposit_all(w, fh, fl):
    high, low = w[0:128, :], w[256:384, :]
    total = dot_rows(fh[...], high) + dot_rows(fl[...], high) + dot_rows(fh[...], low)
    return total.reshape(3, 8, 8, 128)


def flux_x(q, mean_flow):
    return [
        mean_flow * q[0] + q[1],
        mean_flow * q[1] + q[4],
        mean_flow * q[2],
        mean_flow * q[3],
        mean_flow * q[4] + q[1],
    ]


def fluid_rate(state, low_x, high_x, low_y, high_y, mean_flow, cols, mz):
    q = [[state[v, i] for i in range(8)] for v in range(5)]
    both = jnp.concatenate([state[3].reshape(64, 128), state[4].reshape(64, 128)], axis=0)
    high, low = two_parts(both)
    spans = dot_plain(jnp.concatenate([high, low, high], axis=1), mz[...])
    spans = spans.reshape(2, 8, 8, 128)
    node = lax.broadcasted_iota(jnp.int32, (8, 128), 1) & 7
    first, edge = node == 0, LIFT * flag((node == 0) | (node == 7))
    flow = [flux_x([q[v][i] for v in range(5)], mean_flow) for i in range(8)]
    lows = [low_x[v] for v in range(5)]
    highs = [high_x[v] for v in range(5)]
    flow_low, flow_high = flux_x(lows, mean_flow), flux_x(highs, mean_flow)
    first_y, last_y = cols[17], cols[18]
    half_first, half_last = 0.5 * first_y, 0.5 * last_y
    result = [[None] * 8 for _ in range(5)]
    for i in range(8):
        below = [row(low_y[v], i) for v in range(5)]
        above = [row(high_y[v], i) for v in range(5)]
        slopes = {}
        for v in (2, 4):
            value = q[v][i]
            slope = half_first * (below[v] - value) - half_last * (above[v] - value)
            for j in range(8):
                slope = slope + cols[8 + j] * row(value, j)
            slopes[v] = slope
        for v in range(5):
            value = q[v][i]
            total = -float(DERIV[i, 0]) * flow[0][v]
            for b in range(1, 8):
                if DERIV[i, b] != 0.0:
                    total = total - float(DERIV[i, b]) * flow[b][v]
            if i == 0:
                total = total + (0.5 * LIFT) * (flow_low[v] - flow[0][v])
                total = total - LIFT * (value - lows[v])
            if i == 7:
                total = total - (0.5 * LIFT) * (flow_high[v] - flow[7][v])
                total = total + LIFT * (highs[v] - value)
            total = total + first_y * (below[v] - value) + last_y * (above[v] - value)
            if v in (0, 4):
                total = total + slopes[2]
            if v == 2:
                total = total + slopes[4]
            beside = jnp.where(first, pltpu.roll(value, 1, 1), pltpu.roll(value, 127, 1))
            total = total + edge * (beside - value)
            if v in (0, 4):
                total = total + spans[0, i]
            if v == 3:
                total = total + spans[1, i]
            result[v][i] = total
    return result


def droplets_first(planes, cols, w, l1, l2):
    for c in range(8):
        block = planes[c]
        fill_weights(c, block[0:3], block[HOST : HOST + 1], cols, w, l1, l2)


def first_kernel(
    state, low_x, high_x, low_y, high_y, planes, cols_ref, mz,
    state_out, reg_out, forward, x_first, y_first, y_last, drop_out,
    w, s, l1, l2, fh, fl,
):
    cols = [cols_ref[t] for t in range(cols_ref.shape[0])]
    mean_flow = mean_profile(cols)
    droplets_first(planes, cols, w, l1, l2)
    sample_all(state, mean_flow, w, s)
    seat = lax.broadcasted_iota(jnp.int32, (128, 128), 0).astype(F32)
    records, seats = [], []
    for c in range(8):
        block = planes[c]
        fluid = fluid_rows(c, s, l1, l2)
        accel = (fluid - block[3:6]) / block[TAU : TAU + 1]
        register = STEP_SIZE * accel
        velocity = block[3:6] + COEF_B[0] * register
        drop_out[c] = jnp.concatenate([velocity, register, jnp.zeros((2, 128), F32)], axis=0)
        fill_force(c, accel * block[LOAD : LOAD + 1], l1, l2, fh, fl)
        records.append(
            jnp.concatenate(
                [block[0:3], velocity, block[TAU : LOAD + 1], register, jnp.zeros((5, 128), F32)],
                axis=0,
            )
        )
        out_pos = block[OUT_POS : OUT_POS + 1]
        place = jnp.where(out_pos > 0.5, out_pos + float(32 * (c % 4) - 1), -1.0)
        seats.append(flag(seat == place).astype(BF16))
    for g in range(2):
        group = slice(4 * g, 4 * g + 4)
        packed = dot_rows(
            three_parts(jnp.concatenate(records[group], axis=1)),
            jnp.concatenate(seats[group], axis=1),
        )
        packed = packed[0:16] + packed[16:32] + packed[32:48]
        forward[5 + 2 * g] = packed[0:8]
        forward[6 + 2 * g] = packed[8:16]
    source = deposit_all(w, fh, fl)
    rate = fluid_rate(state, low_x, high_x, low_y, high_y, mean_flow, cols, mz)
    for v in range(5):
        for i in range(8):
            total = rate[v][i] + source[v - 1, i] if 1 <= v <= 3 else rate[v][i]
            register = STEP_SIZE * total
            value = state[v, i] + COEF_B[0] * register
            reg_out[v, i] = register
            state_out[v, i] = value
            y_first[v, pl.ds(i, 1), :] = value[0:1]
            y_last[v, pl.ds(i, 1), :] = value[7:8]
            if i == 0:
                x_first[v] = value
            if i == 7:
                forward[v] = value


def second_kernel(
    state, reg_in, low_x, high_x, low_y, high_y, planes, drops, cols_ref, mz,
    state_out, reg_out, back,
    w, s, l1, l2, fh, fl, held,
):
    cols = [cols_ref[t] for t in range(cols_ref.shape[0])]
    mean_flow = mean_profile(cols)
    seat = lax.broadcasted_iota(jnp.int32, (128, 128), 0).astype(F32)
    arrived = []
    for g in range(2):
        packed = jnp.concatenate([low_x[5 + 2 * g], low_x[6 + 2 * g]], axis=0)
        seats = []
        for c in range(4 * g, 4 * g + 4):
            in_pos = planes[c, IN_POS : IN_POS + 1]
            place = jnp.where(in_pos > 0.5, in_pos + float(32 * (c % 4) - 1), -1.0)
            seats.append(flag(seat == place).astype(BF16))
        landed = dot_plain(three_parts(packed), jnp.concatenate(seats, axis=1))
        arrived.append(landed[0:16] + landed[16:32] + landed[32:48])
    for c in range(8):
        block, drop = planes[c], drops[c]
        landed = arrived[c // 4][:, 128 * (c % 4) : 128 * (c % 4) + 128]
        stays = flag(block[OUT_POS : OUT_POS + 1] < 0.5)
        fresh = block[IN_POS : IN_POS + 1] > 0.5
        load = jnp.where(fresh, landed[LOAD : LOAD + 1], block[LOAD : LOAD + 1] * stays)
        live = jnp.where(fresh, 1.0, block[ALIVE : ALIVE + 1] * stays)
        host = jnp.where(fresh, block[IN_HOST : IN_HOST + 1], block[HOST : HOST + 1])
        tau = jnp.where(fresh, landed[TAU : TAU + 1], block[TAU : TAU + 1])
        fresh3 = jnp.broadcast_to(block[IN_POS : IN_POS + 1], (3, 128)) > 0.5
        coords = jnp.where(fresh3, landed[0:3], block[0:3])
        velocity = jnp.where(fresh3, landed[3:6], drop[0:3])
        register = jnp.where(fresh3, landed[8:11], drop[3:6])
        held[c] = jnp.concatenate(
            [velocity, register, tau, load, live, jnp.zeros((7, 128), F32)], axis=0
        )
        fill_weights(c, coords, host, cols, w, l1, l2)
    sample_all(state, mean_flow, w, s)
    for c in range(8):
        block = held[c]
        fluid = fluid_rows(c, s, l1, l2)
        accel = (fluid - block[0:3]) / block[6:7]
        fill_force(c, accel * block[7:8], l1, l2, fh, fl)
        register = COEF_A[1] * block[3:6] + STEP_SIZE * accel
        velocity = block[0:3] + COEF_B[1] * register
        live = block[8:9]
        back[c] = jnp.concatenate(
            [velocity * live, register * live, jnp.zeros((2, 128), F32)], axis=0
        )
    source = deposit_all(w, fh, fl)
    rate = fluid_rate(state, low_x, high_x, low_y, high_y, mean_flow, cols, mz)
    for v in range(5):
        for i in range(8):
            total = rate[v][i] + source[v - 1, i] if 1 <= v <= 3 else rate[v][i]
            register = COEF_A[1] * reg_in[v, i] + STEP_SIZE * total
            reg_out[v, i] = register
            state_out[v, i] = state[v, i] + COEF_B[1] * register


def last_kernel(returned, vel_out, reg_out):
    for a in range(3):
        vel_out[a] = returned[:, a, :]
        reg_out[a] = returned[:, 3 + a, :]


def moved(block, axis, step):
    count = lax.axis_size(axis)
    route = [(i, i + step) for i in range(count) if 0 <= i + step < count]
    return lax.ppermute(block, axis, route)


def shape(*dims):
    return jax.ShapeDtypeStruct(dims, F32)


VMEM = pl.BlockSpec(memory_space=pltpu.VMEM)
SMEM = pl.BlockSpec(memory_space=pltpu.SMEM)
ROOM = pltpu.CompilerParams(vmem_limit_bytes=12 * 1024 * 1024)
WORK = [
    pltpu.VMEM((384, 1024), BF16),
    pltpu.VMEM((192, 1024), F32),
    pltpu.VMEM((8, 1024), F32),
    pltpu.VMEM((8, 1024), F32),
    pltpu.VMEM((192, 1024), BF16),
    pltpu.VMEM((192, 1024), BF16),
]


def local(
    fluid_state,
    drop_xi,
    drop_vel,
    drop_tau,
    drop_mass,
    drop_host,
    drop_alive,
    depart_slots,
    depart_count,
    arrive_slots,
    arrive_host,
    arrive_count,
):
    lanes = depart_slots.shape[-1]
    cols = jnp.asarray(column_planes())
    mz = jnp.asarray(span_matrix())
    face = shape(5, 8, 128)
    payload, x_first, x_last, y_first, y_last = pl.pallas_call(
        send_kernel,
        out_shape=(shape(8, PLANES, 128), face, face, face, face),
        in_specs=[VMEM] * 8 + [SMEM, VMEM, VMEM, SMEM],
        out_specs=(VMEM,) * 5,
        compiler_params=ROOM,
        name="send",
    )(
        fluid_state,
        drop_xi.reshape(3, 8, 128),
        drop_vel.reshape(3, 8, 128),
        drop_tau.reshape(8, 128),
        drop_mass.reshape(8, 128),
        drop_host.reshape(8, 128),
        drop_alive.reshape(8, 128),
        depart_slots.reshape(1, lanes),
        depart_count.reshape(1, 1),
        arrive_slots.reshape(1, lanes),
        arrive_host.reshape(1, lanes),
        arrive_count.reshape(1, 1),
    )
    planes = lax.all_to_all(payload, "cross", split_axis=0, concat_axis=0, tiled=True)
    low_x, high_x = moved(x_last, "stream", 1), moved(x_first, "stream", -1)
    low_y, high_y = moved(y_last, "cross", 1), moved(y_first, "cross", -1)
    state, register, forward, x_first, y_first, y_last, drops = pl.pallas_call(
        first_kernel,
        out_shape=(
            shape(5, 8, 8, 128),
            shape(5, 8, 8, 128),
            shape(9, 8, 128),
            face,
            face,
            face,
            shape(8, 8, 128),
        ),
        in_specs=[VMEM] * 8,
        out_specs=(VMEM,) * 7,
        scratch_shapes=WORK,
        compiler_params=ROOM,
        name="section_1",
    )(fluid_state, low_x, high_x, low_y, high_y, planes, cols, mz)
    low_x, high_x = moved(forward, "stream", 1), moved(x_first, "stream", -1)
    low_y, high_y = moved(y_last, "cross", 1), moved(y_first, "cross", -1)
    state, register, back = pl.pallas_call(
        second_kernel,
        out_shape=(shape(5, 8, 8, 128), shape(5, 8, 8, 128), shape(8, 8, 128)),
        in_specs=[VMEM] * 10,
        out_specs=(VMEM,) * 3,
        scratch_shapes=WORK + [pltpu.VMEM((8, 16, 128), F32)],
        compiler_params=ROOM,
        name="section_2",
    )(state, register, low_x, high_x, low_y, high_y, planes, drops, cols, mz)
    returned = lax.all_to_all(back, "cross", split_axis=0, concat_axis=0, tiled=True)
    velocity, drop_reg = pl.pallas_call(
        last_kernel,
        out_shape=(shape(3, 8, 128), shape(3, 8, 128)),
        in_specs=[VMEM],
        out_specs=(VMEM, VMEM),
        compiler_params=ROOM,
        name="give",
    )(returned)
    return (state, register, velocity.reshape(drop_vel.shape), drop_reg.reshape(drop_vel.shape))


def solution(mesh):
    placed = (
        P(None, "stream", "cross", None),
        P(None, "stream", "cross", None, None),
        P(None, "stream", "cross", None, None),
        P("stream", "cross", None, None),
        P("stream", "cross", None, None),
        P("stream", "cross", None, None),
        P("stream", "cross", None, None),
        P("stream", "cross", None),
        P("stream", "cross"),
        P("stream", "cross", None),
        P("stream", "cross", None),
        P("stream", "cross"),
    )
    return jax.shard_map(
        local,
        mesh=mesh,
        in_specs=placed,
        out_specs=(
            P(None, "stream", "cross", None),
            P(None, "stream", "cross", None),
            P(None, "stream", "cross", None, None),
            P(None, "stream", "cross", None, None),
        ),
        check_vma=False,
    )
```

```python
import jax
import jax.numpy as jnp
import numpy as np
from jax import lax
from jax.experimental import pallas as pl
from jax.experimental.pallas import tpu as pltpu
from jax.sharding import PartitionSpec as P

LIFT = 28.0
STEP_SIZE = 0.02
COEF_A = (0.0, -567301805773.0 / 1357537059087.0)
COEF_B = (1432997174477.0 / 9575080441755.0, 5161836677717.0 / 13612068292357.0)
F32 = jnp.float32
BF16 = jnp.bfloat16

TAU, LOAD, HOST, OUT_POS, IN_POS, IN_HOST, ALIVE = 6, 7, 8, 9, 10, 11, 12
PLANES = 16
FACE = 40


def lgl_tables():
    node_pos = np.array(
        [
            -1.0,
            -0.871740148509607,
            -0.591700181433142,
            -0.209299217902479,
            0.209299217902479,
            0.591700181433142,
            0.871740148509607,
            1.0,
        ]
    )
    bary_wts = np.array(
        [1.0 / np.prod([node_pos[a] - node_pos[b] for b in range(8) if b != a]) for a in range(8)]
    )
    deriv_mat = np.zeros((8, 8))
    for a in range(8):
        for b in range(8):
            if a != b:
                deriv_mat[a, b] = bary_wts[b] / bary_wts[a] / (node_pos[a] - node_pos[b])
        deriv_mat[a, a] = -np.sum(deriv_mat[a])
    return (node_pos, bary_wts, deriv_mat)


NODES, BARY, DERIV = lgl_tables()


def column_planes():
    rows = [BARY]
    rows += [np.roll(NODES, -t) for t in range(1, 8)]
    rows += [-DERIV[:, j] for j in range(8)]
    rows += [0.5 * (1.0 + NODES)]
    rows += [LIFT * (np.arange(8) == 0), LIFT * (np.arange(8) == 7)]
    table = np.stack(rows).astype(np.float32)
    return np.ascontiguousarray(np.broadcast_to(table[:, :, None], table.shape + (128,)))


def span_matrix():
    full = np.zeros((128, 128))
    for e in range(16):
        base = 8 * e
        full[base : base + 8, base : base + 8] -= DERIV.T
        full[(base - 1) % 128, base] += 0.5 * LIFT
        full[base, base] -= 0.5 * LIFT
        full[(base + 8) % 128, base + 7] -= 0.5 * LIFT
        full[base + 7, base + 7] += 0.5 * LIFT
    high = full.astype(np.float32).astype(jnp.bfloat16)
    low = (full - high.astype(np.float64)).astype(np.float32).astype(jnp.bfloat16)
    return np.concatenate([high, high, low], axis=0)


def two_parts(values):
    high = values.astype(BF16)
    return high, (values - high.astype(F32)).astype(BF16)


def three_parts(values):
    high = values.astype(BF16)
    rest = values - high.astype(F32)
    mid = rest.astype(BF16)
    low = (rest - mid.astype(F32)).astype(BF16)
    return jnp.concatenate([high, mid, low], axis=0)


def dot_rows(left, right):
    return lax.dot_general(left, right, (((1,), (1,)), ((), ())), preferred_element_type=F32)


def dot_plain(left, right):
    return lax.dot_general(left, right, (((1,), (0,)), ((), ())), preferred_element_type=F32)


def row(values, index):
    return jnp.broadcast_to(values[index : index + 1], (8, values.shape[1]))


def flag(mask):
    return jnp.where(mask, 1.0, 0.0)


def mean_profile(cols):
    width = float(lax.axis_size("cross"))
    coord_y = lax.axis_index("cross").astype(F32) + cols[16]
    return 0.1 + 0.4 * (1.0 + jnp.tanh(2.0 * (0.25 * width - jnp.abs(coord_y - 0.5 * width))))


def basis(coord_row, cols):
    coord = jnp.broadcast_to(coord_row, (8, 128))
    value = cols[0] * (coord - cols[1])
    for t in range(2, 8):
        value = value * (coord - cols[t])
    return value


def list_planes(dep, dep_count, arr, arr_host, arr_count):
    lanes = dep.shape[1]
    lane = lax.broadcasted_iota(jnp.int32, (1, lanes), 1)
    block_no = lax.broadcasted_iota(jnp.int32, (8, lanes), 0)
    slot_no = lax.broadcasted_iota(jnp.int32, (128, lanes), 0)

    def member(slots, count):
        block = jnp.where(lane < count, slots >> 7, -1)
        return flag(block_no == block)

    dep_in, arr_in = member(dep, dep_count), member(arr, arr_count)
    earlier = flag(
        lax.broadcasted_iota(jnp.int32, (lanes, lanes), 0)
        < lax.broadcasted_iota(jnp.int32, (lanes, lanes), 1)
    ).astype(BF16)
    both = jnp.concatenate([dep_in, arr_in], axis=0)
    ranks = both * (dot_plain(both.astype(BF16), earlier) + 1.0)
    dep_hot = flag(slot_no == (dep & 127)).astype(BF16)
    arr_hot = flag(slot_no == (arr & 127)).astype(BF16)
    out_pos = dot_rows(ranks[:8].astype(BF16), dep_hot)
    arr_rows = jnp.concatenate([ranks[8:], arr_in * arr_host.astype(F32)], axis=0)
    landed = dot_rows(arr_rows.astype(BF16), arr_hot)
    return out_pos, landed[:8], landed[8:]


def put_faces(out, state, first_row):
    me = lax.axis_index("cross")
    low, high = state[:, :, 0, :].reshape(FACE, 128), state[:, :, 7, :].reshape(FACE, 128)
    for b in range(8):
        out[b, pl.ds(first_row, FACE), :] = jnp.where(b > me, high, low)


def take_faces(planes, first_row):
    me, count = lax.axis_index("cross"), lax.axis_size("cross")
    rows = pl.ds(first_row, FACE)
    low = planes[pl.ds(jnp.maximum(me - 1, 0), 1), rows, :].reshape(5, 8, 128)
    high = planes[pl.ds(jnp.minimum(me + 1, count - 1), 1), rows, :].reshape(5, 8, 128)
    return jnp.where(me > 0, low, 0.0), jnp.where(me < count - 1, high, 0.0)


def send_kernel(*refs):
    dep_count, arr_count, sources = refs[0], refs[1], refs[2:12]
    (out, x_first, x_last), held, sem = refs[12:15], refs[15:25], refs[25]
    copies = [pltpu.make_async_copy(sources[k], held[k], sem.at[k]) for k in range(10)]
    for copy in copies:
        copy.start()
    state, xi, vel, tau, mass, host, alive, dep, arr, arr_host = held
    for copy in copies[7:]:
        copy.wait()
    out_pos, in_pos, in_host = list_planes(
        dep[...], dep_count[...], arr[...], arr_host[...], arr_count[...]
    )
    out[:, OUT_POS, :] = out_pos
    out[:, IN_POS, :] = in_pos
    out[:, IN_HOST, :] = in_host
    for copy in copies[:7]:
        copy.wait()
    x_first[...] = state[:, 0]
    x_last[...] = state[:, 7]
    put_faces(out, state, PLANES)
    live = alive[...].astype(F32)
    for a in range(3):
        out[:, a, :] = xi[a]
        out[:, 3 + a, :] = vel[a]
    out[:, TAU, :] = tau[...]
    out[:, LOAD, :] = mass[...] * live
    out[:, HOST, :] = host[...].astype(F32)
    out[:, ALIVE, :] = live
    for r in range(ALIVE + 1, PLANES):
        out[:, r, :] = jnp.zeros((8, 128), F32)


def fill_weights(c, coords, host_row, cols, w, l1, l2):
    lanes = pl.ds(128 * c, 128)
    l1[:, lanes] = basis(coords[0:1], cols)
    l2[:, lanes] = basis(coords[1:2], cols)
    third = basis(coords[2:3], cols)
    high = third.astype(BF16).astype(F32)
    low = third - high
    host = jnp.broadcast_to(host_row, (8, 128))
    zero = jnp.zeros((8, 128), F32)
    for e in range(0, 16, 2):
        here, after = host == float(e), host == float(e + 1)
        rows_h = jnp.concatenate(
            [jnp.where(here, high, zero), jnp.where(after, high, zero)], axis=0
        ).astype(BF16)
        rows_l = jnp.concatenate(
            [jnp.where(here, low, zero), jnp.where(after, low, zero)], axis=0
        ).astype(BF16)
        w[pl.ds(8 * e, 16), lanes] = rows_h
        w[pl.ds(128 + 8 * e, 16), lanes] = rows_h
        w[pl.ds(256 + 8 * e, 16), lanes] = rows_l


def sample_all(state, mean_flow, w, s):
    fields = jnp.concatenate([state[1] + mean_flow[None], state[2], state[3]], axis=0)
    high, low = two_parts(fields.reshape(192, 128))
    s[...] = dot_plain(jnp.concatenate([high, low, high], axis=1), w[...])


def fluid_rows(c, s, l1, l2):
    lanes = pl.ds(128 * c, 128)
    along_x, along_y = l1[:, lanes], l2[:, lanes]
    rows = []
    for a in range(3):
        total = None
        for i in range(8):
            term = row(along_x, i) * s[pl.ds(64 * a + 8 * i, 8), lanes]
            total = term if total is None else total + term
        rows.append(jnp.sum(total * along_y, axis=0, keepdims=True))
    return jnp.concatenate(rows, axis=0)


def fill_force(c, force, l1, l2, fh, fl):
    lanes = pl.ds(128 * c, 128)
    along_x, along_y = l1[:, lanes], l2[:, lanes]
    pushes = [-row(force, a) for a in range(3)]
    for i in range(0, 8, 2):
        plane = jnp.concatenate([row(along_x, i) * along_y, row(along_x, i + 1) * along_y], axis=0)
        for a in range(3):
            high, low = two_parts(plane * jnp.concatenate([pushes[a], pushes[a]], axis=0))
            fh[pl.ds(64 * a + 8 * i, 16), lanes] = high
            fl[pl.ds(64 * a + 8 * i, 16), lanes] = low


def deposit_all(w, fh, fl):
    high, low = w[0:128, :], w[256:384, :]
    total = dot_rows(fh[...], high) + dot_rows(fl[...], high) + dot_rows(fh[...], low)
    return total.reshape(3, 8, 8, 128)


def flux_x(q, mean_flow):
    return [
        mean_flow * q[0] + q[1],
        mean_flow * q[1] + q[4],
        mean_flow * q[2],
        mean_flow * q[3],
        mean_flow * q[4] + q[1],
    ]


def inner_rate(state, mean_flow, cols, mz):
    q = [[state[v, i] for i in range(8)] for v in range(5)]
    both = jnp.concatenate([state[3].reshape(64, 128), state[4].reshape(64, 128)], axis=0)
    high, low = two_parts(both)
    spans = dot_plain(jnp.concatenate([high, low, high], axis=1), mz[...])
    spans = spans.reshape(2, 8, 8, 128)
    node = lax.broadcasted_iota(jnp.int32, (8, 128), 1) & 7
    first, edge = node == 0, LIFT * flag((node == 0) | (node == 7))
    flow = [flux_x([q[v][i] for v in range(5)], mean_flow) for i in range(8)]
    ends_y = cols[17] + cols[18]
    half_y = 0.5 * (cols[18] - cols[17])
    result = [[None] * 8 for _ in range(5)]
    for i in range(8):
        slopes = {}
        for v in (2, 4):
            value = q[v][i]
            slope = half_y * value
            for j in range(8):
                slope = slope + cols[8 + j] * row(value, j)
            slopes[v] = slope
        for v in range(5):
            value = q[v][i]
            factors = -DERIV[i]
            if i == 0:
                factors = factors - 0.5 * LIFT * (np.arange(8) == 0)
            if i == 7:
                factors = factors + 0.5 * LIFT * (np.arange(8) == 7)
            total = None
            for b in range(8):
                if factors[b] != 0.0:
                    term = float(factors[b]) * flow[b][v]
                    total = term if total is None else total + term
            if i in (0, 7):
                total = total - LIFT * value
            total = total - ends_y * value
            if v in (0, 4):
                total = total + slopes[2]
            if v == 2:
                total = total + slopes[4]
            beside = jnp.where(first, pltpu.roll(value, 1, 1), pltpu.roll(value, 127, 1))
            total = total + edge * (beside - value)
            if v in (0, 4):
                total = total + spans[0, i]
            if v == 3:
                total = total + spans[1, i]
            result[v][i] = total
    return result


def outer_rate(low_x, high_x, low_y, high_y, mean_flow, cols):
    first_y, last_y = cols[17], cols[18]
    lows, highs = [low_x[v] for v in range(5)], [high_x[v] for v in range(5)]
    flow_low, flow_high = flux_x(lows, mean_flow), flux_x(highs, mean_flow)
    result = [[None] * 8 for _ in range(5)]
    for i in range(8):
        below = [row(low_y[v], i) for v in range(5)]
        above = [row(high_y[v], i) for v in range(5)]
        flux = {0: 2, 2: 4, 4: 2}
        for v in range(5):
            at_first, at_last = below[v], above[v]
            if v in flux:
                at_first = at_first + 0.5 * below[flux[v]]
                at_last = at_last - 0.5 * above[flux[v]]
            total = first_y * at_first + last_y * at_last
            if i == 0:
                total = total + (0.5 * LIFT) * flow_low[v] + LIFT * lows[v]
            if i == 7:
                total = total - (0.5 * LIFT) * flow_high[v] + LIFT * highs[v]
            result[v][i] = total
    return result


def droplets_first(planes, cols, w, l1, l2):
    for c in range(8):
        block = planes[c, 0:PLANES]
        fill_weights(c, block[0:3], block[HOST : HOST + 1], cols, w, l1, l2)


def first_kernel(
    state, low_x, high_x, planes, cols_ref, mz,
    state_out, reg_out, forward, drop_out,
    w, s, l1, l2, fh, fl,
):
    cols = [cols_ref[t] for t in range(cols_ref.shape[0])]
    mean_flow = mean_profile(cols)
    droplets_first(planes, cols, w, l1, l2)
    sample_all(state, mean_flow, w, s)
    seat = lax.broadcasted_iota(jnp.int32, (128, 128), 0).astype(F32)
    records, seats = [], []
    for c in range(8):
        block = planes[c, 0:PLANES]
        fluid = fluid_rows(c, s, l1, l2)
        accel = (fluid - block[3:6]) / block[TAU : TAU + 1]
        register = STEP_SIZE * accel
        velocity = block[3:6] + COEF_B[0] * register
        drop_out[c] = jnp.concatenate([velocity, register, jnp.zeros((2, 128), F32)], axis=0)
        fill_force(c, accel * block[LOAD : LOAD + 1], l1, l2, fh, fl)
        records.append(
            jnp.concatenate(
                [block[0:3], velocity, block[TAU : LOAD + 1], register, jnp.zeros((5, 128), F32)],
                axis=0,
            )
        )
        out_pos = block[OUT_POS : OUT_POS + 1]
        place = jnp.where(out_pos > 0.5, out_pos + float(32 * (c % 4) - 1), -1.0)
        seats.append(flag(seat == place).astype(BF16))
    for g in range(2):
        group = slice(4 * g, 4 * g + 4)
        packed = dot_rows(
            three_parts(jnp.concatenate(records[group], axis=1)),
            jnp.concatenate(seats[group], axis=1),
        )
        packed = packed[0:16] + packed[16:32] + packed[32:48]
        forward[5 + 2 * g] = packed[0:8]
        forward[6 + 2 * g] = packed[8:16]
    source = deposit_all(w, fh, fl)
    low_y, high_y = take_faces(planes, PLANES)
    rate = inner_rate(state, mean_flow, cols, mz)
    extra = outer_rate(low_x, high_x, low_y, high_y, mean_flow, cols)
    for v in range(5):
        for i in range(8):
            total = rate[v][i] + extra[v][i]
            if 1 <= v <= 3:
                total = total + source[v - 1, i]
            register = STEP_SIZE * total
            value = state[v, i] + COEF_B[0] * register
            reg_out[v, i] = register
            state_out[v, i] = value
            if i == 7:
                forward[v] = value


def sample_kernel(
    state, packed_in, planes, drops, cols_ref,
    back, x_first, w, fh, fl,
    s, l1, l2, held,
):
    cols = [cols_ref[t] for t in range(cols_ref.shape[0])]
    mean_flow = mean_profile(cols)
    seat = lax.broadcasted_iota(jnp.int32, (128, 128), 0).astype(F32)
    arrived = []
    for g in range(2):
        packed = jnp.concatenate([packed_in[5 + 2 * g], packed_in[6 + 2 * g]], axis=0)
        seats = []
        for c in range(4 * g, 4 * g + 4):
            in_pos = planes[c, IN_POS : IN_POS + 1]
            place = jnp.where(in_pos > 0.5, in_pos + float(32 * (c % 4) - 1), -1.0)
            seats.append(flag(seat == place).astype(BF16))
        landed = dot_plain(three_parts(packed), jnp.concatenate(seats, axis=1))
        arrived.append(landed[0:16] + landed[16:32] + landed[32:48])
    for c in range(8):
        block, drop = planes[c, 0:PLANES], drops[c]
        landed = arrived[c // 4][:, 128 * (c % 4) : 128 * (c % 4) + 128]
        stays = flag(block[OUT_POS : OUT_POS + 1] < 0.5)
        fresh = block[IN_POS : IN_POS + 1] > 0.5
        load = jnp.where(fresh, landed[LOAD : LOAD + 1], block[LOAD : LOAD + 1] * stays)
        live = jnp.where(fresh, 1.0, block[ALIVE : ALIVE + 1] * stays)
        host = jnp.where(fresh, block[IN_HOST : IN_HOST + 1], block[HOST : HOST + 1])
        tau = jnp.where(fresh, landed[TAU : TAU + 1], block[TAU : TAU + 1])
        fresh3 = jnp.broadcast_to(block[IN_POS : IN_POS + 1], (3, 128)) > 0.5
        coords = jnp.where(fresh3, landed[0:3], block[0:3])
        velocity = jnp.where(fresh3, landed[3:6], drop[0:3])
        register = jnp.where(fresh3, landed[8:11], drop[3:6])
        held[c] = jnp.concatenate(
            [velocity, register, tau, load, live, jnp.zeros((7, 128), F32)], axis=0
        )
        fill_weights(c, coords, host, cols, w, l1, l2)
    sample_all(state, mean_flow, w, s)
    for c in range(8):
        block = held[c]
        fluid = fluid_rows(c, s, l1, l2)
        accel = (fluid - block[0:3]) / block[6:7]
        fill_force(c, accel * block[7:8], l1, l2, fh, fl)
        register = COEF_A[1] * block[3:6] + STEP_SIZE * accel
        velocity = block[0:3] + COEF_B[1] * register
        live = block[8:9]
        back[c, 0:8] = jnp.concatenate(
            [velocity * live, register * live, jnp.zeros((2, 128), F32)], axis=0
        )
    put_faces(back, state, 8)
    x_first[...] = state[:, 0]


def inner_kernel(state, reg_in, w, fh, fl, cols_ref, mz, state_out, reg_out):
    cols = [cols_ref[t] for t in range(cols_ref.shape[0])]
    source = deposit_all(w, fh, fl)
    rate = inner_rate(state, mean_profile(cols), cols, mz)
    for v in range(5):
        for i in range(8):
            total = rate[v][i] + source[v - 1, i] if 1 <= v <= 3 else rate[v][i]
            register = COEF_A[1] * reg_in[v, i] + STEP_SIZE * total
            reg_out[v, i] = register
            state_out[v, i] = state[v, i] + COEF_B[1] * register


def last_kernel(
    state, reg_in, low_x, high_x, returned, cols_ref, state_out, reg_out, vel_out, drop_out
):
    cols = [cols_ref[t] for t in range(cols_ref.shape[0])]
    low_y, high_y = take_faces(returned, 8)
    extra = outer_rate(low_x, high_x, low_y, high_y, mean_profile(cols), cols)
    for v in range(5):
        for i in range(8):
            register = STEP_SIZE * extra[v][i]
            reg_out[v, i] = reg_in[v, i] + register
            state_out[v, i] = state[v, i] + COEF_B[1] * register
    for a in range(3):
        vel_out[a] = returned[:, a, :]
        drop_out[a] = returned[:, 3 + a, :]


def moved(block, axis, step):
    count = lax.axis_size(axis)
    route = [(i, i + step) for i in range(count) if 0 <= i + step < count]
    return lax.ppermute(block, axis, route)


def shape(*dims):
    return jax.ShapeDtypeStruct(dims, F32)


VMEM = pl.BlockSpec(memory_space=pltpu.VMEM)
HBM = pl.BlockSpec(memory_space=pltpu.HBM)
ROOM = pltpu.CompilerParams(vmem_limit_bytes=12 * 1024 * 1024)
FULL = pltpu.CompilerParams(vmem_limit_bytes=60 * 1024 * 1024)
WEIGHTS = (384, 1024)
FORCES = (192, 1024)
WORK = [pltpu.VMEM((192, 1024), F32), pltpu.VMEM((8, 1024), F32), pltpu.VMEM((8, 1024), F32)]


def local(
    fluid_state,
    drop_xi,
    drop_vel,
    drop_tau,
    drop_mass,
    drop_host,
    drop_alive,
    depart_slots,
    depart_count,
    arrive_slots,
    arrive_host,
    arrive_count,
):
    lanes = depart_slots.shape[-1]
    cols = jnp.asarray(column_planes())
    mz = jnp.asarray(span_matrix())
    face, whole = shape(5, 8, 128), shape(5, 8, 8, 128)
    arguments = (
        fluid_state,
        drop_xi.reshape(3, 8, 128),
        drop_vel.reshape(3, 8, 128),
        drop_tau.reshape(8, 128),
        drop_mass.reshape(8, 128),
        drop_host.reshape(8, 128),
        drop_alive.reshape(8, 128),
        depart_slots.reshape(1, lanes),
        arrive_slots.reshape(1, lanes),
        arrive_host.reshape(1, lanes),
    )
    counts = (depart_count.reshape(1, 1), arrive_count.reshape(1, 1))
    payload, x_first, x_last = pl.pallas_call(
        send_kernel,
        out_shape=(shape(8, PLANES + FACE, 128), face, face),
        in_specs=[VMEM] * 2 + [HBM] * 10,
        out_specs=(VMEM,) * 3,
        scratch_shapes=[pltpu.VMEM(a.shape, a.dtype) for a in arguments]
        + [pltpu.SemaphoreType.DMA((10,))],
        compiler_params=FULL,
        name="send",
    )(*counts, *arguments)
    planes = lax.all_to_all(payload, "cross", split_axis=0, concat_axis=0, tiled=True)
    low_x, high_x = moved(x_last, "stream", 1), moved(x_first, "stream", -1)
    state, register, forward, drops = pl.pallas_call(
        first_kernel,
        out_shape=(whole, whole, shape(9, 8, 128), shape(8, 8, 128)),
        in_specs=[VMEM] * 6,
        out_specs=(VMEM,) * 4,
        scratch_shapes=[pltpu.VMEM(WEIGHTS, BF16)] + WORK + [pltpu.VMEM(FORCES, BF16)] * 2,
        compiler_params=ROOM,
        name="section_1",
    )(fluid_state, low_x, high_x, planes, cols, mz)
    low_x = moved(forward, "stream", 1)
    back, x_first, w, fh, fl = pl.pallas_call(
        sample_kernel,
        out_shape=(
            shape(8, 8 + FACE, 128),
            face,
            jax.ShapeDtypeStruct(WEIGHTS, BF16),
            jax.ShapeDtypeStruct(FORCES, BF16),
            jax.ShapeDtypeStruct(FORCES, BF16),
        ),
        in_specs=[VMEM] * 5,
        out_specs=(VMEM,) * 5,
        scratch_shapes=WORK + [pltpu.VMEM((8, 16, 128), F32)],
        compiler_params=ROOM,
        name="sample_2",
    )(state, low_x, planes, drops, cols)
    returned = lax.all_to_all(back, "cross", split_axis=0, concat_axis=0, tiled=True)
    high_x = moved(x_first, "stream", -1)
    state, register = pl.pallas_call(
        inner_kernel,
        out_shape=(whole, whole),
        in_specs=[VMEM] * 7,
        out_specs=(VMEM,) * 2,
        compiler_params=ROOM,
        name="inner_2",
    )(state, register, w, fh, fl, cols, mz)
    state, register, velocity, drop_reg = pl.pallas_call(
        last_kernel,
        out_shape=(whole, whole, shape(3, 8, 128), shape(3, 8, 128)),
        in_specs=[VMEM] * 6,
        out_specs=(VMEM,) * 4,
        compiler_params=ROOM,
        name="last",
    )(state, register, low_x, high_x, returned, cols)
    return (state, register, velocity.reshape(drop_vel.shape), drop_reg.reshape(drop_vel.shape))


def solution(mesh):
    placed = (
        P(None, "stream", "cross", None),
        P(None, "stream", "cross", None, None),
        P(None, "stream", "cross", None, None),
        P("stream", "cross", None, None),
        P("stream", "cross", None, None),
        P("stream", "cross", None, None),
        P("stream", "cross", None, None),
        P("stream", "cross", None),
        P("stream", "cross"),
        P("stream", "cross", None),
        P("stream", "cross", None),
        P("stream", "cross"),
    )
    return jax.shard_map(
        local,
        mesh=mesh,
        in_specs=placed,
        out_specs=(
            P(None, "stream", "cross", None),
            P(None, "stream", "cross", None),
            P(None, "stream", "cross", None, None),
            P(None, "stream", "cross", None, None),
        ),
        check_vma=False,
    )
```

```python
import jax
import jax.numpy as jnp
import numpy as np
from jax import lax
from jax.experimental import pallas as pl
from jax.experimental.pallas import tpu as pltpu
from jax.sharding import PartitionSpec as P

LIFT = 28.0
STEP_SIZE = 0.02
COEF_A = (0.0, -567301805773.0 / 1357537059087.0)
COEF_B = (1432997174477.0 / 9575080441755.0, 5161836677717.0 / 13612068292357.0)
F32 = jnp.float32
BF16 = jnp.bfloat16

TAU, LOAD, HOST, OUT_POS, IN_POS, IN_HOST, ALIVE = 6, 7, 8, 9, 10, 11, 12
PLANES = 16
FACE = 40


def lgl_tables():
    node_pos = np.array(
        [
            -1.0,
            -0.871740148509607,
            -0.591700181433142,
            -0.209299217902479,
            0.209299217902479,
            0.591700181433142,
            0.871740148509607,
            1.0,
        ]
    )
    bary_wts = np.array(
        [1.0 / np.prod([node_pos[a] - node_pos[b] for b in range(8) if b != a]) for a in range(8)]
    )
    deriv_mat = np.zeros((8, 8))
    for a in range(8):
        for b in range(8):
            if a != b:
                deriv_mat[a, b] = bary_wts[b] / bary_wts[a] / (node_pos[a] - node_pos[b])
        deriv_mat[a, a] = -np.sum(deriv_mat[a])
    return (node_pos, bary_wts, deriv_mat)


NODES, BARY, DERIV = lgl_tables()


def column_planes():
    rows = [BARY]
    rows += [np.roll(NODES, -t) for t in range(1, 8)]
    rows += [-DERIV[:, j] for j in range(8)]
    rows += [0.5 * (1.0 + NODES)]
    rows += [LIFT * (np.arange(8) == 0), LIFT * (np.arange(8) == 7)]
    table = np.stack(rows).astype(np.float32)
    return np.ascontiguousarray(np.broadcast_to(table[:, :, None], table.shape + (128,)))


def span_matrix():
    full = np.zeros((128, 128))
    for e in range(16):
        base = 8 * e
        full[base : base + 8, base : base + 8] -= DERIV.T
        full[(base - 1) % 128, base] += 0.5 * LIFT
        full[base, base] -= 0.5 * LIFT
        full[(base + 8) % 128, base + 7] -= 0.5 * LIFT
        full[base + 7, base + 7] += 0.5 * LIFT
    high = full.astype(np.float32).astype(jnp.bfloat16)
    low = (full - high.astype(np.float64)).astype(np.float32).astype(jnp.bfloat16)
    return np.concatenate([high, high, low], axis=0)


def two_parts(values):
    high = values.astype(BF16)
    return high, (values - high.astype(F32)).astype(BF16)


def three_parts(values):
    high = values.astype(BF16)
    rest = values - high.astype(F32)
    mid = rest.astype(BF16)
    low = (rest - mid.astype(F32)).astype(BF16)
    return jnp.concatenate([high, mid, low], axis=0)


def dot_rows(left, right):
    return lax.dot_general(left, right, (((1,), (1,)), ((), ())), preferred_element_type=F32)


def dot_plain(left, right):
    return lax.dot_general(left, right, (((1,), (0,)), ((), ())), preferred_element_type=F32)


def row(values, index):
    return jnp.broadcast_to(values[index : index + 1], (8, values.shape[1]))


def flag(mask):
    return jnp.where(mask, 1.0, 0.0)


def mean_profile(cols):
    width = float(lax.axis_size("cross"))
    coord_y = lax.axis_index("cross").astype(F32) + cols[16]
    return 0.1 + 0.4 * (1.0 + jnp.tanh(2.0 * (0.25 * width - jnp.abs(coord_y - 0.5 * width))))


def basis(coord_row, cols):
    coord = jnp.broadcast_to(coord_row, (8, 128))
    value = cols[0] * (coord - cols[1])
    for t in range(2, 8):
        value = value * (coord - cols[t])
    return value


def list_planes(dep, dep_count, arr, arr_host, arr_count):
    lanes = dep.shape[1]
    lane = lax.broadcasted_iota(jnp.int32, (1, lanes), 1)
    block_no = lax.broadcasted_iota(jnp.int32, (8, lanes), 0)
    slot_no = lax.broadcasted_iota(jnp.int32, (128, lanes), 0)

    def member(slots, count):
        block = jnp.where(lane < count, slots >> 7, -1)
        return flag(block_no == block)

    dep_in, arr_in = member(dep, dep_count), member(arr, arr_count)
    earlier = flag(
        lax.broadcasted_iota(jnp.int32, (lanes, lanes), 0)
        < lax.broadcasted_iota(jnp.int32, (lanes, lanes), 1)
    ).astype(BF16)
    both = jnp.concatenate([dep_in, arr_in], axis=0)
    ranks = both * (dot_plain(both.astype(BF16), earlier) + 1.0)
    dep_hot = flag(slot_no == (dep & 127)).astype(BF16)
    arr_hot = flag(slot_no == (arr & 127)).astype(BF16)
    out_pos = dot_rows(ranks[:8].astype(BF16), dep_hot)
    arr_rows = jnp.concatenate([ranks[8:], arr_in * arr_host.astype(F32)], axis=0)
    landed = dot_rows(arr_rows.astype(BF16), arr_hot)
    return out_pos, landed[:8], landed[8:]


def put_faces(out, state, first_row):
    me = lax.axis_index("cross")
    low, high = state[:, :, 0, :].reshape(FACE, 128), state[:, :, 7, :].reshape(FACE, 128)
    for b in range(8):
        out[b, pl.ds(first_row, FACE), :] = jnp.where(b > me, high, low)


def take_faces(planes, first_row):
    me, count = lax.axis_index("cross"), lax.axis_size("cross")
    rows = pl.ds(first_row, FACE)
    low = planes[pl.ds(jnp.maximum(me - 1, 0), 1), rows, :].reshape(5, 8, 128)
    high = planes[pl.ds(jnp.minimum(me + 1, count - 1), 1), rows, :].reshape(5, 8, 128)
    return jnp.where(me > 0, low, 0.0), jnp.where(me < count - 1, high, 0.0)


def send_kernel(*refs):
    dep_count, arr_count, sources = refs[0], refs[1], refs[2:12]
    (out, x_first), held, sem = refs[12:14], refs[14:24], refs[24]
    copies = [pltpu.make_async_copy(sources[k], held[k], sem.at[k]) for k in range(10)]
    for copy in copies:
        copy.start()
    state, xi, vel, tau, mass, host, alive, dep, arr, arr_host = held
    for copy in copies[7:]:
        copy.wait()
    out_pos, in_pos, in_host = list_planes(
        dep[...], dep_count[...], arr[...], arr_host[...], arr_count[...]
    )
    out[:, OUT_POS, :] = out_pos
    out[:, IN_POS, :] = in_pos
    out[:, IN_HOST, :] = in_host
    for copy in copies[:7]:
        copy.wait()
    x_first[...] = state[:, 0]
    put_faces(out, state, PLANES)
    live = alive[...].astype(F32)
    for a in range(3):
        out[:, a, :] = xi[a]
        out[:, 3 + a, :] = vel[a]
    out[:, TAU, :] = tau[...]
    out[:, LOAD, :] = mass[...] * live
    out[:, HOST, :] = host[...].astype(F32)
    out[:, ALIVE, :] = live
    for r in range(ALIVE + 1, PLANES):
        out[:, r, :] = jnp.zeros((8, 128), F32)


def fill_weights(c, coords, host_row, cols, w, l1, l2):
    lanes = pl.ds(128 * c, 128)
    l1[:, lanes] = basis(coords[0:1], cols)
    l2[:, lanes] = basis(coords[1:2], cols)
    third = basis(coords[2:3], cols)
    high = third.astype(BF16).astype(F32)
    low = third - high
    host = jnp.broadcast_to(host_row, (8, 128))
    zero = jnp.zeros((8, 128), F32)
    for e in range(0, 16, 2):
        here, after = host == float(e), host == float(e + 1)
        rows_h = jnp.concatenate(
            [jnp.where(here, high, zero), jnp.where(after, high, zero)], axis=0
        ).astype(BF16)
        rows_l = jnp.concatenate(
            [jnp.where(here, low, zero), jnp.where(after, low, zero)], axis=0
        ).astype(BF16)
        w[pl.ds(8 * e, 16), lanes] = rows_h
        w[pl.ds(128 + 8 * e, 16), lanes] = rows_h
        w[pl.ds(256 + 8 * e, 16), lanes] = rows_l


def sample_all(state, mean_flow, w, s):
    fields = jnp.concatenate([state[1] + mean_flow[None], state[2], state[3]], axis=0)
    high, low = two_parts(fields.reshape(192, 128))
    s[...] = dot_plain(jnp.concatenate([high, low, high], axis=1), w[...])


def fluid_rows(c, s, l1, l2):
    lanes = pl.ds(128 * c, 128)
    along_x, along_y = l1[:, lanes], l2[:, lanes]
    rows = []
    for a in range(3):
        total = None
        for i in range(8):
            term = row(along_x, i) * s[pl.ds(64 * a + 8 * i, 8), lanes]
            total = term if total is None else total + term
        rows.append(jnp.sum(total * along_y, axis=0, keepdims=True))
    return jnp.concatenate(rows, axis=0)


def fill_force(c, force, l1, l2, fh, fl):
    lanes = pl.ds(128 * c, 128)
    along_x, along_y = l1[:, lanes], l2[:, lanes]
    pushes = [-row(force, a) for a in range(3)]
    for i in range(0, 8, 2):
        plane = jnp.concatenate([row(along_x, i) * along_y, row(along_x, i + 1) * along_y], axis=0)
        for a in range(3):
            high, low = two_parts(plane * jnp.concatenate([pushes[a], pushes[a]], axis=0))
            fh[pl.ds(64 * a + 8 * i, 16), lanes] = high
            fl[pl.ds(64 * a + 8 * i, 16), lanes] = low


def deposit_all(w, fh, fl):
    high, low = w[0:128, :], w[256:384, :]
    total = dot_rows(fh[...], high) + dot_rows(fl[...], high) + dot_rows(fh[...], low)
    return total.reshape(3, 8, 8, 128)


def flux_x(q, mean_flow):
    return [
        mean_flow * q[0] + q[1],
        mean_flow * q[1] + q[4],
        mean_flow * q[2],
        mean_flow * q[3],
        mean_flow * q[4] + q[1],
    ]


def inner_rate(state, mean_flow, cols, mz):
    q = [[state[v, i] for i in range(8)] for v in range(5)]
    both = jnp.concatenate([state[3].reshape(64, 128), state[4].reshape(64, 128)], axis=0)
    high, low = two_parts(both)
    spans = dot_plain(jnp.concatenate([high, low, high], axis=1), mz[...])
    spans = spans.reshape(2, 8, 8, 128)
    node = lax.broadcasted_iota(jnp.int32, (8, 128), 1) & 7
    first, edge = node == 0, LIFT * flag((node == 0) | (node == 7))
    flow = [flux_x([q[v][i] for v in range(5)], mean_flow) for i in range(8)]
    ends_y = cols[17] + cols[18]
    half_y = 0.5 * (cols[18] - cols[17])
    result = [[None] * 8 for _ in range(5)]
    for i in range(8):
        slopes = {}
        for v in (2, 4):
            value = q[v][i]
            slope = half_y * value
            for j in range(8):
                slope = slope + cols[8 + j] * row(value, j)
            slopes[v] = slope
        for v in range(5):
            value = q[v][i]
            factors = -DERIV[i]
            if i == 0:
                factors = factors - 0.5 * LIFT * (np.arange(8) == 0)
            if i == 7:
                factors = factors + 0.5 * LIFT * (np.arange(8) == 7)
            total = None
            for b in range(8):
                if factors[b] != 0.0:
                    term = float(factors[b]) * flow[b][v]
                    total = term if total is None else total + term
            if i in (0, 7):
                total = total - LIFT * value
            total = total - ends_y * value
            if v in (0, 4):
                total = total + slopes[2]
            if v == 2:
                total = total + slopes[4]
            beside = jnp.where(first, pltpu.roll(value, 1, 1), pltpu.roll(value, 127, 1))
            total = total + edge * (beside - value)
            if v in (0, 4):
                total = total + spans[0, i]
            if v == 3:
                total = total + spans[1, i]
            result[v][i] = total
    return result


def lift_first(face, mean_flow):
    flow = flux_x(face, mean_flow)
    return [(0.5 * LIFT) * flow[v] + LIFT * face[v] for v in range(5)]


def lift_last(face, mean_flow):
    flow = flux_x(face, mean_flow)
    return [LIFT * face[v] - (0.5 * LIFT) * flow[v] for v in range(5)]


def lifts_y(low_y, high_y, cols):
    first_y, last_y = cols[17], cols[18]
    flux = {0: 2, 2: 4, 4: 2}
    result = [[None] * 8 for _ in range(5)]
    for i in range(8):
        below = [row(low_y[v], i) for v in range(5)]
        above = [row(high_y[v], i) for v in range(5)]
        for v in range(5):
            at_first, at_last = below[v], above[v]
            if v in flux:
                at_first = at_first + 0.5 * below[flux[v]]
                at_last = at_last - 0.5 * above[flux[v]]
            result[v][i] = first_y * at_first + last_y * at_last
    return result


def droplets_first(planes, cols, w, l1, l2):
    for c in range(8):
        block = planes[c, 0:PLANES]
        fill_weights(c, block[0:3], block[HOST : HOST + 1], cols, w, l1, l2)


def first_kernel(
    state, rate, planes, cols_ref,
    state_out, reg_out, forward, drop_out,
    w, s, l1, l2, fh, fl,
):
    cols = [cols_ref[t] for t in range(cols_ref.shape[0])]
    mean_flow = mean_profile(cols)
    droplets_first(planes, cols, w, l1, l2)
    sample_all(state, mean_flow, w, s)
    seat = lax.broadcasted_iota(jnp.int32, (128, 128), 0).astype(F32)
    records, seats = [], []
    for c in range(8):
        block = planes[c, 0:PLANES]
        fluid = fluid_rows(c, s, l1, l2)
        accel = (fluid - block[3:6]) / block[TAU : TAU + 1]
        register = STEP_SIZE * accel
        velocity = block[3:6] + COEF_B[0] * register
        drop_out[c] = jnp.concatenate([velocity, register, jnp.zeros((2, 128), F32)], axis=0)
        fill_force(c, accel * block[LOAD : LOAD + 1], l1, l2, fh, fl)
        records.append(
            jnp.concatenate(
                [block[0:3], velocity, block[TAU : LOAD + 1], register, jnp.zeros((5, 128), F32)],
                axis=0,
            )
        )
        out_pos = block[OUT_POS : OUT_POS + 1]
        place = jnp.where(out_pos > 0.5, out_pos + float(32 * (c % 4) - 1), -1.0)
        seats.append(flag(seat == place).astype(BF16))
    for g in range(2):
        group = slice(4 * g, 4 * g + 4)
        packed = dot_rows(
            three_parts(jnp.concatenate(records[group], axis=1)),
            jnp.concatenate(seats[group], axis=1),
        )
        packed = packed[0:16] + packed[16:32] + packed[32:48]
        forward[10 + 2 * g] = packed[0:8]
        forward[11 + 2 * g] = packed[8:16]
    source = deposit_all(w, fh, fl)
    low_y, high_y = take_faces(planes, PLANES)
    extra = lifts_y(low_y, high_y, cols)
    for v in range(5):
        forward[v] = state[v, 7]
        for i in range(8):
            total = rate[v, i] + extra[v][i]
            if 1 <= v <= 3:
                total = total + source[v - 1, i]
            register = STEP_SIZE * total
            value = state[v, i] + COEF_B[0] * register
            reg_out[v, i] = register
            state_out[v, i] = value
            if i == 7:
                forward[5 + v] = value


def sample_kernel(
    state_in, reg_in, behind, ahead, planes, drops, cols_ref,
    state, reg, back, x_first, w, l1, l2, force,
    s, held,
):
    cols = [cols_ref[t] for t in range(cols_ref.shape[0])]
    mean_flow = mean_profile(cols)
    lifts = {
        0: lift_first([behind[v] for v in range(5)], mean_flow),
        7: lift_last([ahead[v] for v in range(5)], mean_flow),
    }
    for v in range(5):
        for i in range(8):
            if i in lifts:
                register = STEP_SIZE * lifts[i][v]
                reg[v, i] = reg_in[v, i] + register
                state[v, i] = state_in[v, i] + COEF_B[0] * register
            else:
                reg[v, i] = reg_in[v, i]
                state[v, i] = state_in[v, i]
    seat = lax.broadcasted_iota(jnp.int32, (128, 128), 0).astype(F32)
    arrived = []
    for g in range(2):
        packed = jnp.concatenate([behind[10 + 2 * g], behind[11 + 2 * g]], axis=0)
        seats = []
        for c in range(4 * g, 4 * g + 4):
            in_pos = planes[c, IN_POS : IN_POS + 1]
            place = jnp.where(in_pos > 0.5, in_pos + float(32 * (c % 4) - 1), -1.0)
            seats.append(flag(seat == place).astype(BF16))
        landed = dot_plain(three_parts(packed), jnp.concatenate(seats, axis=1))
        arrived.append(landed[0:16] + landed[16:32] + landed[32:48])
    for c in range(8):
        block, drop = planes[c, 0:PLANES], drops[c]
        landed = arrived[c // 4][:, 128 * (c % 4) : 128 * (c % 4) + 128]
        stays = flag(block[OUT_POS : OUT_POS + 1] < 0.5)
        fresh = block[IN_POS : IN_POS + 1] > 0.5
        load = jnp.where(fresh, landed[LOAD : LOAD + 1], block[LOAD : LOAD + 1] * stays)
        live = jnp.where(fresh, 1.0, block[ALIVE : ALIVE + 1] * stays)
        host = jnp.where(fresh, block[IN_HOST : IN_HOST + 1], block[HOST : HOST + 1])
        tau = jnp.where(fresh, landed[TAU : TAU + 1], block[TAU : TAU + 1])
        fresh3 = jnp.broadcast_to(block[IN_POS : IN_POS + 1], (3, 128)) > 0.5
        coords = jnp.where(fresh3, landed[0:3], block[0:3])
        velocity = jnp.where(fresh3, landed[3:6], drop[0:3])
        register = jnp.where(fresh3, landed[8:11], drop[3:6])
        held[c] = jnp.concatenate(
            [velocity, register, tau, load, live, jnp.zeros((7, 128), F32)], axis=0
        )
        fill_weights(c, coords, host, cols, w, l1, l2)
    sample_all(state, mean_flow, w, s)
    for c in range(8):
        block = held[c]
        fluid = fluid_rows(c, s, l1, l2)
        accel = (fluid - block[0:3]) / block[6:7]
        force[c, 0:3] = accel * block[7:8]
        register = COEF_A[1] * block[3:6] + STEP_SIZE * accel
        velocity = block[0:3] + COEF_B[1] * register
        live = block[8:9]
        back[c, 0:8] = jnp.concatenate(
            [velocity * live, register * live, jnp.zeros((2, 128), F32)], axis=0
        )
    put_faces(back, state, 8)
    x_first[...] = state[:, 0]


def rate_kernel(state, cols_ref, mz, rate_out):
    cols = [cols_ref[t] for t in range(cols_ref.shape[0])]
    rate = inner_rate(state, mean_profile(cols), cols, mz)
    for v in range(5):
        for i in range(8):
            rate_out[v, i] = rate[v][i]


def inner_kernel(
    state, reg_in, start, behind, w, l1, l2, force, cols_ref, mz, state_out, reg_out, fh, fl
):
    cols = [cols_ref[t] for t in range(cols_ref.shape[0])]
    mean_flow = mean_profile(cols)
    added = lift_last([start[v, 0] for v in range(5)], mean_flow)
    factor = jnp.where(lax.axis_index("stream") > 0, STEP_SIZE * COEF_B[0], 0.0)
    lifts = {0: lift_first([behind[5 + v] + factor * added[v] for v in range(5)], mean_flow)}
    for c in range(8):
        fill_force(c, force[c, 0:3], l1, l2, fh, fl)
    source = deposit_all(w, fh, fl)
    rate = inner_rate(state, mean_flow, cols, mz)
    for v in range(5):
        for i in range(8):
            total = rate[v][i] + source[v - 1, i] if 1 <= v <= 3 else rate[v][i]
            if i in lifts:
                total = total + lifts[i][v]
            register = COEF_A[1] * reg_in[v, i] + STEP_SIZE * total
            reg_out[v, i] = register
            state_out[v, i] = state[v, i] + COEF_B[1] * register


def last_kernel(state, reg_in, ahead, returned, cols_ref, state_out, reg_out, vel_out, drop_out):
    cols = [cols_ref[t] for t in range(cols_ref.shape[0])]
    low_y, high_y = take_faces(returned, 8)
    extra = lifts_y(low_y, high_y, cols)
    lifts = {7: lift_last([ahead[v] for v in range(5)], mean_profile(cols))}
    for v in range(5):
        for i in range(8):
            total = extra[v][i] + lifts[i][v] if i in lifts else extra[v][i]
            register = STEP_SIZE * total
            reg_out[v, i] = reg_in[v, i] + register
            state_out[v, i] = state[v, i] + COEF_B[1] * register
    for a in range(3):
        vel_out[a] = returned[:, a, :]
        drop_out[a] = returned[:, 3 + a, :]


def moved(block, axis, step):
    count = lax.axis_size(axis)
    route = [(i, i + step) for i in range(count) if 0 <= i + step < count]
    return lax.ppermute(block, axis, route)


def shape(*dims):
    return jax.ShapeDtypeStruct(dims, F32)


VMEM = pl.BlockSpec(memory_space=pltpu.VMEM)
HBM = pl.BlockSpec(memory_space=pltpu.HBM)
ROOM = pltpu.CompilerParams(vmem_limit_bytes=12 * 1024 * 1024)
FULL = pltpu.CompilerParams(vmem_limit_bytes=60 * 1024 * 1024)
WEIGHTS = (384, 1024)
FORCES = (192, 1024)
WORK = [pltpu.VMEM((192, 1024), F32), pltpu.VMEM((8, 1024), F32), pltpu.VMEM((8, 1024), F32)]


def local(
    fluid_state,
    drop_xi,
    drop_vel,
    drop_tau,
    drop_mass,
    drop_host,
    drop_alive,
    depart_slots,
    depart_count,
    arrive_slots,
    arrive_host,
    arrive_count,
):
    lanes = depart_slots.shape[-1]
    cols = jnp.asarray(column_planes())
    mz = jnp.asarray(span_matrix())
    face, whole = shape(5, 8, 128), shape(5, 8, 8, 128)
    arguments = (
        fluid_state,
        drop_xi.reshape(3, 8, 128),
        drop_vel.reshape(3, 8, 128),
        drop_tau.reshape(8, 128),
        drop_mass.reshape(8, 128),
        drop_host.reshape(8, 128),
        drop_alive.reshape(8, 128),
        depart_slots.reshape(1, lanes),
        arrive_slots.reshape(1, lanes),
        arrive_host.reshape(1, lanes),
    )
    counts = (depart_count.reshape(1, 1), arrive_count.reshape(1, 1))
    payload, x_first = pl.pallas_call(
        send_kernel,
        out_shape=(shape(8, PLANES + FACE, 128), face),
        in_specs=[VMEM] * 2 + [HBM] * 10,
        out_specs=(VMEM, VMEM),
        scratch_shapes=[pltpu.VMEM(a.shape, a.dtype) for a in arguments]
        + [pltpu.SemaphoreType.DMA((10,))],
        compiler_params=FULL,
        name="send",
    )(*counts, *arguments)
    planes = lax.all_to_all(payload, "cross", split_axis=0, concat_axis=0, tiled=True)
    ahead = moved(x_first, "stream", -1)
    rate = pl.pallas_call(
        rate_kernel,
        out_shape=whole,
        in_specs=[VMEM] * 3,
        out_specs=VMEM,
        compiler_params=ROOM,
        name="inner_1",
    )(fluid_state, cols, mz)
    state, register, forward, drops = pl.pallas_call(
        first_kernel,
        out_shape=(whole, whole, shape(14, 8, 128), shape(8, 8, 128)),
        in_specs=[VMEM] * 4,
        out_specs=(VMEM,) * 4,
        scratch_shapes=[pltpu.VMEM(WEIGHTS, BF16)] + WORK + [pltpu.VMEM(FORCES, BF16)] * 2,
        compiler_params=ROOM,
        name="section_1",
    )(fluid_state, rate, planes, cols)
    behind = moved(forward, "stream", 1)
    state, register, back, x_first, w, l1, l2, force = pl.pallas_call(
        sample_kernel,
        out_shape=(
            whole,
            whole,
            shape(8, 8 + FACE, 128),
            face,
            jax.ShapeDtypeStruct(WEIGHTS, BF16),
            shape(8, 1024),
            shape(8, 1024),
            shape(8, 8, 128),
        ),
        in_specs=[VMEM] * 7,
        out_specs=(VMEM,) * 8,
        scratch_shapes=WORK[:1] + [pltpu.VMEM((8, 16, 128), F32)],
        compiler_params=ROOM,
        name="sample_2",
    )(state, register, behind, ahead, planes, drops, cols)
    returned = lax.all_to_all(back, "cross", split_axis=0, concat_axis=0, tiled=True)
    ahead = moved(x_first, "stream", -1)
    state, register = pl.pallas_call(
        inner_kernel,
        out_shape=(whole, whole),
        in_specs=[VMEM] * 10,
        out_specs=(VMEM,) * 2,
        scratch_shapes=[pltpu.VMEM(FORCES, BF16)] * 2,
        compiler_params=ROOM,
        name="inner_2",
    )(state, register, fluid_state, behind, w, l1, l2, force, cols, mz)
    state, register, velocity, drop_reg = pl.pallas_call(
        last_kernel,
        out_shape=(whole, whole, shape(3, 8, 128), shape(3, 8, 128)),
        in_specs=[VMEM] * 5,
        out_specs=(VMEM,) * 4,
        compiler_params=ROOM,
        name="last",
    )(state, register, ahead, returned, cols)
    return (state, register, velocity.reshape(drop_vel.shape), drop_reg.reshape(drop_vel.shape))


def solution(mesh):
    placed = (
        P(None, "stream", "cross", None),
        P(None, "stream", "cross", None, None),
        P(None, "stream", "cross", None, None),
        P("stream", "cross", None, None),
        P("stream", "cross", None, None),
        P("stream", "cross", None, None),
        P("stream", "cross", None, None),
        P("stream", "cross", None),
        P("stream", "cross"),
        P("stream", "cross", None),
        P("stream", "cross", None),
        P("stream", "cross"),
    )
    return jax.shard_map(
        local,
        mesh=mesh,
        in_specs=placed,
        out_specs=(
            P(None, "stream", "cross", None),
            P(None, "stream", "cross", None),
            P(None, "stream", "cross", None, None),
            P(None, "stream", "cross", None, None),
        ),
        check_vma=False,
    )
```
